1024 devices in a mesh: dp: 64 (over z, y_lo), expert: 8 (over x, y_hi), tensor: 2 (over core).
Axes of the slice: x: 4, y: 4 (y_hi: 2, y_lo: 2; y = y_hi * 2 + y_lo), z: 32, core: 2. Of those that a mesh axis runs over, the one named last changes fastest.
Arguments:
- tokens: bfloat16 [65536, 4096], P(('dp', 'expert')), may hold values from -6 to 6
- grads_out: bfloat16 [65536, 4096], P(('dp', 'expert')), may hold values from -6 to 6
- expert_ids: int32 [65536, 1], P(('dp', 'expert')), may hold values from 0 to 7; in each aligned block of 128 rows (0 to 127, 128 to 255, ...) at most 20 rows name the same one
- gate_weights: float32 [65536, 1], P(('dp', 'expert')), may hold values from 0.1 to 0.9
- layout_map: int32 [65536], P(('dp', 'expert')), may hold values from 0 to 127, as said below
- gate_w: bfloat16 [8, 4096, 768], P('expert', None, 'tensor'), may hold values from -0.09375 to 0.09375
- up_w: bfloat16 [8, 4096, 768], P('expert', None, 'tensor'), may hold values from -0.09375 to 0.09375
- down_w: bfloat16 [8, 768, 4096], P('expert', 'tensor'), may hold values from -0.21875 to 0.21875
Outputs:
- layer_out: bfloat16 [65536, 4096], P(('dp', 'expert', 'tensor'))
- input_grad: bfloat16 [65536, 4096], P(('dp', 'expert', 'tensor'))
The draws below stay inside these ranges and needn't reach their ends.
Inputs may be any that keep to these rules, and one draw needn't show every extreme that they name: `expert_ids`: each row names one expert. Within each aligned block of 128 rows (the tokens of one index of dp and expert) no expert is named by more than 20 rows, a bound that some block reaches. `layout_map`: within each aligned block of 128 tokens the values are a permutation of 0 to 127.
All inputs are finite; a program needn't handle non-finite values.
Results may differ from the reference program's by a relative error of at most 0.0065.
Values may be sent and summed in bfloat16 or wider, within the bound.
A program may use at most 64 MiB of HBM per device.

```python
import math
import jax
import jax.numpy as jnp
import numpy as np
from jax import lax

D = 4096
HID = 768
TOP = 1
TOK = 128
EXPERTS = 8
CAP = 20
TOKENS = 65536
N_TENSOR = 2


def draw_layout_map(key, part):
    blocks = TOKENS // TOK
    block_keys = jax.random.split(key, blocks)

    def draw_block(block_key):
        return jax.random.permutation(block_key, TOK)
    return jax.vmap(draw_block)(block_keys).reshape(TOKENS).astype(jnp.int32)


def shard_levels(stream_key, shape, cuts, smallest, high):
    loudness, own = 1.0, jax.random.fold_in(stream_key, 6)
    for position, blocks in cuts:
        steps = jnp.exp(jax.random.uniform(jax.random.fold_in(own, position), (blocks,), jnp.float32, smallest / len(cuts), high / len(cuts)))
        loudness = loudness * jnp.repeat(steps, shape[position] // blocks).reshape([-1 if axis == position else 1 for axis in range(len(shape))])
    return loudness


def shared_out(stream_key, own, number, rows, amount, top, limit, slope):
    order = jax.random.permutation(stream_key, amount)
    crowded, ordinary = shares(amount, rows * top, limit, slope, True), shares(amount, rows * top, limit, slope, False)
    places = jnp.arange(amount)

    def named(lengths, turn):
        used = int((lengths > 0).sum())
        fixed = max(1, used // 4)
        moved = fixed + (places - fixed + turn * (used - fixed)) % max(1, amount - fixed)
        return jnp.zeros((amount,), jnp.int32).at[order[jnp.where(places < fixed, places, moved)]].set(jnp.asarray(lengths, jnp.int32))

    lengths = jnp.where(number % 4 == 0, named(crowded, number // 4), named(ordinary, number - number // 4 - 1))
    mixed = jax.random.permutation(jax.random.fold_in(own, 3), amount)
    source_of, sink = mixed[0:amount // 2 * 2:2], mixed[1:amount // 2 * 2:2]
    slack = jnp.minimum(lengths[source_of] - 1, limit - lengths[sink]) // 2
    slack = jnp.where((source_of == order[0]) | (sink == order[0]) | (lengths[sink] == 0), 0, jnp.maximum(slack, 0))
    moved = jax.random.randint(jax.random.fold_in(own, 4), (amount // 2,), 0, 1 << 20) % (slack + 1)
    lengths = lengths.at[source_of].add(-moved).at[sink].add(moved)
    labels = jnp.searchsorted(jnp.cumsum(lengths), jnp.arange(rows * top), side="right").astype(jnp.int32)
    grid = labels.reshape(top, rows).T
    grid = grid[jax.random.permutation(jax.random.fold_in(own, 1), rows)]
    turn = jax.random.randint(jax.random.fold_in(own, 2), (rows, 1), 0, top)
    return jnp.take_along_axis(grid, (jnp.arange(top)[None, :] + turn) % top, axis=1)


def shares(number_of, total, most, skew, full):
    weights = [(1 << 20) // math.isqrt(grade ** skew) + 1 for grade in range(1, number_of + 1)]
    largest = most if full else min(most, max(-(-total // number_of), total * weights[0] // sum(weights)))
    least = 1 if total - largest >= number_of - 1 else 0
    given, rest = [largest] + [least] * (number_of - 1), total - largest - least * (number_of - 1)
    while rest > 0:
        candidates = [i for i in range(1, number_of) if given[i] < largest] or [i for i in range(1, number_of) if given[i] < most]
        mass, remaining = sum([weights[i] for i in candidates]), rest
        for i in candidates:
            addition = min(most - given[i], max(1, remaining * weights[i] // mass), rest)
            given[i] = given[i] + addition
            rest = rest - addition
    return np.array(given)


def scatter_about(own_key, dims, deviation, limit, cuts=(), kind=jnp.bfloat16):
    values = deviation * jax.random.normal(own_key, dims, jnp.float32)
    if cuts:
        values = values * shard_levels(own_key, dims, cuts, -0.22, 0.18)
    return jnp.clip(values, -limit, limit).astype(kind)


def setup_inputs(seed: int = 0) -> dict:
    key_of = jax.random.split(jax.random.key(seed), 9)
    tokens = scatter_about(key_of[0], (TOKENS, D), 1.0, 6.0, ((0, 512),))
    grads_out = scatter_about(key_of[1], (TOKENS, D), 1.0, 6.0, ((0, 512),))
    expert_ids_keys = jax.random.split(jax.random.fold_in(key_of[2], 1), TOKENS // TOK)
    expert_ids_turns = jax.random.permutation(jax.random.fold_in(key_of[2], 3), TOKENS // TOK)
    expert_ids = jax.vmap(lambda own, number: shared_out(jax.random.fold_in(key_of[2], 2), own, number, TOK, EXPERTS, TOP, CAP, 2))(expert_ids_keys, expert_ids_turns).reshape((TOKENS, TOP))
    gate_weights = jnp.clip(0.1 + 0.79999997 * jax.random.uniform(key_of[3], (TOKENS, TOP), jnp.float32) ** shard_levels(key_of[3], (TOKENS, TOP), ((0, 512),), -0.2, 0.2), 0.1, 0.9)
    layout_map = draw_layout_map(jax.random.fold_in(key_of[8], 71), 0)
    gate_w = scatter_about(key_of[5], (EXPERTS, D, HID), D ** -0.5, 0.09375, ((0, 8), (2, 2)))
    up_w = scatter_about(key_of[6], (EXPERTS, D, HID), D ** -0.5, 0.09375, ((0, 8), (2, 2)))
    down_w = scatter_about(key_of[7], (EXPERTS, HID, D), HID ** -0.5, 0.21875, ((0, 8), (1, 2)))
    return dict(tokens=tokens, grads_out=grads_out, expert_ids=expert_ids, gate_weights=gate_weights, layout_map=layout_map, gate_w=gate_w, up_w=up_w, down_w=down_w)


def reference(tokens, grads_out, expert_ids, gate_weights, layout_map, gate_w, up_w, down_w):
    groups = TOKENS // TOK
    pair_count = TOK * TOP
    slot_count = EXPERTS * CAP
    flat_ids = expert_ids.reshape(groups, pair_count)
    onehot = (flat_ids[:, :, None] == jnp.arange(EXPERTS, dtype=jnp.int32)[None, None, :]).astype(jnp.int32)
    before = jnp.cumsum(onehot, axis=1) - onehot
    slot_rank = jnp.sum(before * onehot, axis=2)
    slot_index = flat_ids * CAP + slot_rank
    slot_match = (slot_index[:, None, :] == jnp.arange(slot_count, dtype=jnp.int32)[None, :, None]).astype(jnp.int32)
    pair_index = jnp.sum(slot_match * jnp.arange(pair_count, dtype=jnp.int32)[None, None, :], axis=2)
    is_filled = jnp.sum(slot_match, axis=2)
    source_token = jnp.arange(groups, dtype=jnp.int32)[:, None] * TOK + pair_index // TOP
    slot_gate = jnp.take_along_axis(gate_weights.reshape(groups, pair_count), pair_index, axis=1) * is_filled.astype(jnp.float32)

    def by_expert(table):
        return jnp.transpose(table.reshape(groups, EXPERTS, CAP), (1, 0, 2)).reshape(EXPERTS, groups * CAP)

    rows_all = by_expert(source_token)
    gates_all = by_expert(slot_gate)
    filled_all = by_expert(is_filled)
    hidden_part = HID // N_TENSOR

    def per_expert(carry, inputs):
        out_acc, grad_acc = carry
        w_gate, w_up, w_down, rows, gates, filled = inputs
        expert_in = tokens[rows] * filled.astype(jnp.bfloat16)[:, None]
        grad_in = (grads_out[rows].astype(jnp.float32) * gates[:, None]).astype(jnp.bfloat16)
        out_total = jnp.zeros((rows.shape[0], D), jnp.float32)
        grad_total = jnp.zeros((rows.shape[0], D), jnp.float32)
        for part_index in range(N_TENSOR):
            lower = part_index * hidden_part
            gate_cols = w_gate[:, lower:lower + hidden_part]
            up_cols = w_up[:, lower:lower + hidden_part]
            down_rows = w_down[lower:lower + hidden_part, :]
            pre_gate = jnp.dot(expert_in, gate_cols, preferred_element_type=jnp.float32)
            pre_up = jnp.dot(expert_in, up_cols, preferred_element_type=jnp.float32)
            sigma = jax.nn.sigmoid(pre_gate)
            active = pre_gate * sigma
            hidden = (active * pre_up).astype(jnp.bfloat16)
            part_out = jnp.dot(hidden, down_rows, preferred_element_type=jnp.float32).astype(jnp.bfloat16)
            grad_hidden = jnp.dot(grad_in, down_rows.T, preferred_element_type=jnp.float32)
            grad_gate = (grad_hidden * pre_up * sigma * (1.0 + pre_gate * (1.0 - sigma))).astype(jnp.bfloat16)
            grad_up = (grad_hidden * active).astype(jnp.bfloat16)
            part_grad = (jnp.dot(grad_gate, gate_cols.T, preferred_element_type=jnp.float32)
                         + jnp.dot(grad_up, up_cols.T, preferred_element_type=jnp.float32)).astype(jnp.bfloat16)
            out_total = out_total + part_out.astype(jnp.float32)
            grad_total = grad_total + part_grad.astype(jnp.float32)
        slot_out = lax.optimization_barrier(out_total.astype(jnp.bfloat16)).astype(jnp.float32)
        slot_grad = lax.optimization_barrier(grad_total.astype(jnp.bfloat16)).astype(jnp.float32)
        out_acc = out_acc.at[rows].add(slot_out * gates[:, None])
        grad_acc = grad_acc.at[rows].add(slot_grad * filled.astype(jnp.float32)[:, None])
        return (out_acc, grad_acc), None

    start = (jnp.zeros((TOKENS, D), jnp.float32), jnp.zeros((TOKENS, D), jnp.float32))
    (out_acc, grad_acc), unused = lax.scan(per_expert, start, (gate_w, up_w, down_w, rows_all, gates_all, filled_all))
    token_out = out_acc.astype(jnp.bfloat16)
    token_grad = grad_acc.astype(jnp.bfloat16)
    target = (jnp.arange(TOKENS, dtype=jnp.int32) // TOK) * TOK + layout_map
    layer_out = jnp.zeros((TOKENS, D), jnp.bfloat16).at[target].set(token_out)
    input_grad = jnp.zeros((TOKENS, D), jnp.bfloat16).at[target].set(token_grad)
    return (layer_out, input_grad)
```

```python
import functools

import jax
import jax.numpy as jnp
from jax import lax
from jax.experimental import pallas as pl
from jax.experimental.pallas import tpu as pltpu
from jax.sharding import PartitionSpec as P

MESH = pl.DeviceIdType.MESH
BF, F32 = jnp.bfloat16, jnp.float32


def iota(shape, axis):
    return lax.broadcasted_iota(jnp.int32, shape, axis)


def dot(a, b):
    return jnp.dot(a, b, preferred_element_type=F32)


def dot_t(a, b):
    return lax.dot_general(a, b, (((1,), (1,)), ((), ())), preferred_element_type=F32)


def one_hot(mask):
    return jnp.where(mask, 1.0, 0.0).astype(BF)


def kernel(
    experts, cap,
    ids_ref, gates_ref, layout_ref, tokens_ref, grads_ref, wg_hbm, wu_hbm, wd_hbm,
    out_ref, grad_ref,
    rows, send_main, send_left, x_all, left_all, wg, wu, wd,
    pre_gate, pre_up, hidden, grad_gate, grad_up, part_away, part_home, part_recv,
    back_main, back_left, home_main, home_left, pick_main, pick_left, gate_row, away_out,
    in_sem, w_sem, disp_s, disp_r, fwd_s, fwd_r, part_s, part_r, ret_s, ret_r, end_s, end_r,
):
    me, core = lax.axis_index("expert"), lax.axis_index("tensor")
    tok, width = tokens_ref.shape
    half = width // 2
    quarter = half // 4
    peers = experts - 1
    main = 16 * experts
    extra = cap - 16
    half_rows = tok // 2
    partner = {"tensor": 1 - core}
    mine = pl.multiple_of(core * half, 128)
    other = pl.multiple_of((1 - core) * half, 128)

    def peer(k):
        x, y = me // 2, me % 2
        return ((x + k // 2) % (experts // 2)) * 2 + (y + k) % 2

    def source(k):
        x, y = me // 2, me % 2
        return ((x + experts // 2 - k // 2) % (experts // 2)) * 2 + (y + k) % 2

    barrier = pltpu.get_barrier_semaphore()
    for k in range(1, experts):
        pl.semaphore_signal(barrier, inc=1, device_id={"expert": peer(k)}, device_id_type=MESH)
    pl.semaphore_signal(barrier, inc=1, device_id=partner, device_id_type=MESH)

    loads = [
        pltpu.make_async_copy(tokens_ref.at[:, pl.ds(mine, half)], rows.at[0], in_sem.at[0]),
        pltpu.make_async_copy(grads_ref.at[:, pl.ds(mine, half)], rows.at[1], in_sem.at[1]),
    ]
    weights = [
        pltpu.make_async_copy(wg_hbm, wg, w_sem.at[0]),
        pltpu.make_async_copy(wu_hbm, wu, w_sem.at[1]),
        pltpu.make_async_copy(wd_hbm, wd, w_sem.at[2]),
    ]
    for copy in loads + weights:
        copy.start()

    ids = ids_ref[...]
    named = one_hot(iota((experts, tok), 0) == ids)
    earlier = one_hot(iota((tok, tok), 0) < iota((tok, tok), 1))
    rank = jnp.sum(dot(named, earlier) * named.astype(F32), axis=0, keepdims=True)
    base = ids.astype(F32) * 16.0
    row_id = iota((main, tok), 0).astype(F32)
    main_row = jnp.where(rank < 16.0, base + rank, -1.0)
    to_main = one_hot(row_id == main_row)
    to_left = []
    for q in range(4):
        left_row = jnp.where(rank < 16.0, -1.0, base + (rank - 16.0 + extra * q))
        to_left.append(one_hot(row_id == left_row))
    gates = gates_ref[...]
    same = iota((tok, tok), 0) == iota((tok, tok), 1)
    gate_col = jnp.sum(jnp.where(same, gates, 0.0), axis=1, keepdims=True)

    def dispatch(a, k):
        e = peer(k)
        here, there = pl.ds(pl.multiple_of(e * 16, 16), 16), pl.ds(pl.multiple_of(me * 16, 16), 16)
        return (
            pltpu.make_async_remote_copy(
                send_main.at[a, here], x_all.at[a, there, pl.ds(mine, half)],
                disp_s.at[a, k, 0], disp_r.at[a, k, 0], device_id={"expert": e}, device_id_type=MESH),
            pltpu.make_async_remote_copy(
                send_left.at[a, here], left_all.at[a, core, there],
                disp_s.at[a, k, 1], disp_r.at[a, k, 1], device_id={"expert": e}, device_id_type=MESH),
        )

    def forward(a, k):
        at = pl.ds(pl.multiple_of(source(k) * 16, 16), 16)
        return (
            pltpu.make_async_remote_copy(
                x_all.at[a, at, pl.ds(mine, half)], x_all.at[a, at, pl.ds(mine, half)],
                fwd_s.at[a, k, 0], fwd_r.at[a, k, 0], device_id=partner, device_id_type=MESH),
            pltpu.make_async_remote_copy(
                left_all.at[a, core, at], left_all.at[a, core, at],
                fwd_s.at[a, k, 1], fwd_r.at[a, k, 1], device_id=partner, device_id_type=MESH),
        )

    def arrange(a):
        left = jnp.zeros((main, quarter), F32)
        for q in range(4):
            cols = pl.ds(q * quarter, quarter)
            block = rows[a, :, cols]
            if a == 1:
                block = (block.astype(F32) * gate_col).astype(BF)
            send_main[a, :, cols] = dot(to_main, block).astype(BF)
            left = left + dot(to_left[q], block)
        send_left[a] = left.astype(BF)

    def send_all(a):
        for k in range(1, experts):
            for copy in dispatch(a, k):
                copy.start()
        own = pl.ds(pl.multiple_of(me * 16, 16), 16)
        x_all[a, own, pl.ds(mine, half)] = send_main[a, own]
        left_all[a, core, own] = send_left[a, own]

    def forward_all(a):
        for copy in forward(a, 0):
            copy.start()
        for k in range(1, experts):
            for copy in dispatch(a, k):
                copy.wait_recv()
            for copy in forward(a, k):
                copy.start()

    def forward_wait(a):
        for k in range(experts):
            for copy in forward(a, k):
                copy.wait_recv()

    def spread_left(a):
        r, c = iota((experts * extra, main), 0), iota((experts * extra, main), 1)
        for q in range(4):
            pick = one_hot(c == (r // extra) * 16 + q * extra + r % extra)
            for h in range(2):
                x_all[a, main:, pl.ds(h * half + q * quarter, quarter)] = dot(pick, left_all[a, h]).astype(BF)

    loads[0].wait()
    arrange(0)
    pl.semaphore_wait(barrier, peers + 1)
    send_all(0)
    loads[1].wait()
    arrange(1)
    send_all(1)

    place = one_hot(iota((tok, tok), 0) == layout_ref[...])
    pick_main[...] = dot_t(place, to_main).astype(BF)
    for q in range(4):
        pick_left[q] = dot_t(place, to_left[q]).astype(BF)
    gate_row[...] = jnp.sum(jnp.where(iota((tok, tok), 0) == layout_ref[...], gates, 0.0), axis=1, keepdims=True)

    forward_all(0)
    for copy in weights:
        copy.wait()
    forward_wait(0)
    spread_left(0)
    pre_gate[...] = dot(x_all[0], wg[...])
    pre_up[...] = dot(x_all[0], wu[...])
    hidden[...] = (pre_gate[...] * jax.nn.sigmoid(pre_gate[...]) * pre_up[...]).astype(BF)
    forward_all(1)

    def exchange(a):
        return pltpu.make_async_remote_copy(
            part_away.at[a], part_recv.at[a], part_s.at[a], part_r.at[a], device_id=partner, device_id_type=MESH)

    def out_part(start, ref):
        for q in range(4):
            cols = pl.ds(q * quarter, quarter)
            ref[0, :, cols] = dot(hidden[...], wd[:, pl.ds(pl.multiple_of(start + q * quarter, 128), quarter)]).astype(BF)

    def grad_part(start, ref):
        for q in range(4):
            cols = pl.ds(q * quarter, quarter)
            at = pl.ds(pl.multiple_of(start + q * quarter, 128), quarter)
            ref[1, :, cols] = (dot_t(grad_gate[...], wg[at, :]) + dot_t(grad_up[...], wu[at, :])).astype(BF)

    def give_back(a, k):
        g = peer(k)
        here, there = pl.ds(pl.multiple_of(g * 16, 16), 16), pl.ds(pl.multiple_of(me * 16, 16), 16)
        return (
            pltpu.make_async_remote_copy(
                back_main.at[a, here], home_main.at[a, there],
                ret_s.at[a, k, 0], ret_r.at[a, k, 0], device_id={"expert": g}, device_id_type=MESH),
            pltpu.make_async_remote_copy(
                back_left.at[a, here], home_left.at[a, there],
                ret_s.at[a, k, 1], ret_r.at[a, k, 1], device_id={"expert": g}, device_id_type=MESH),
        )

    def return_all(a):
        exchange(a).wait_recv()
        r, c = iota((main, experts * extra), 0), iota((main, experts * extra), 1)
        packed = jnp.zeros((main, quarter), F32)
        for q in range(4):
            cols = pl.ds(q * quarter, quarter)
            total = (part_home[a, :, cols].astype(F32) + part_recv[a, :, cols].astype(F32)).astype(BF)
            back_main[a, :, cols] = total[:main]
            pick = one_hot(r == (c // extra) * 16 + q * extra + c % extra)
            packed = packed + dot(pick, total[main:])
        back_left[a] = packed.astype(BF)
        for k in range(1, experts):
            for copy in give_back(a, k):
                copy.start()
        own = pl.ds(pl.multiple_of(me * 16, 16), 16)
        home_main[a, own] = back_main[a, own]
        home_left[a, own] = back_left[a, own]

    out_part(other, part_away)
    exchange(0).start()
    out_part(mine, part_home)
    forward_wait(1)
    spread_left(1)
    return_all(0)

    grad_hidden = dot_t(x_all[1], wd[...])
    gate_v, up_v = pre_gate[...], pre_up[...]
    sigma = jax.nn.sigmoid(gate_v)
    grad_gate[...] = (grad_hidden * up_v * sigma * (1.0 + gate_v * (1.0 - sigma))).astype(BF)
    grad_up[...] = (grad_hidden * gate_v * sigma).astype(BF)
    grad_part(other, part_away)
    exchange(1).start()
    grad_part(mine, part_home)
    return_all(1)

    def finish_copy(a, ref):
        return pltpu.make_async_remote_copy(
            away_out.at[a], ref.at[:, pl.ds(mine, half)], end_s.at[a], end_r.at[a],
            device_id=partner, device_id_type=MESH)

    keep = pl.ds(pl.multiple_of(core * half_rows, half_rows), half_rows)
    give = pl.ds(pl.multiple_of((1 - core) * half_rows, half_rows), half_rows)

    def finish(a, ref):
        for k in range(1, experts):
            for copy in give_back(a, k):
                copy.wait_recv()

        def placed(at, q):
            cols = pl.ds(q * quarter, quarter)
            value = dot(pick_main[at], home_main[a, :, cols]) + dot(pick_left[q, at], home_left[a])
            if a == 0:
                value = value * gate_row[at]
            return value.astype(BF)

        for q in range(4):
            away_out[a, :, pl.ds(q * quarter, quarter)] = placed(give, q)
        finish_copy(a, ref).start()
        for q in range(4):
            ref[:, pl.ds(pl.multiple_of(mine + q * quarter, 128), quarter)] = placed(keep, q)

    finish(0, out_ref)
    finish(1, grad_ref)

    for a, ref in ((0, out_ref), (1, grad_ref)):
        for k in range(1, experts):
            for copy in dispatch(a, k):
                copy.wait_send()
            for copy in give_back(a, k):
                copy.wait_send()
        for k in range(experts):
            for copy in forward(a, k):
                copy.wait_send()
        exchange(a).wait_send()
        finish_copy(a, ref).wait()


def shards(tokens, grads_out, expert_ids, gate_weights, layout_map, gate_w, up_w, down_w):
    tok, width = tokens.shape
    experts = lax.axis_size("expert")
    hid = gate_w.shape[2]
    cap = tok * 5 // (4 * experts)
    half = width // 2
    quarter = half // 4
    slots, main = experts * cap, experts * 16
    vmem, dma = pltpu.VMEM, pltpu.SemaphoreType.DMA
    in_vmem, anywhere = pl.BlockSpec(memory_space=pltpu.VMEM), pl.BlockSpec(memory_space=pl.ANY)
    out = jax.ShapeDtypeStruct((tok // 2, width), BF)
    return pl.pallas_call(
        functools.partial(kernel, experts, cap),
        out_shape=(out, out),
        in_specs=[in_vmem] * 3 + [anywhere] * 5,
        out_specs=(in_vmem, in_vmem),
        scratch_shapes=[
            vmem((2, tok, half), BF),
            vmem((2, main, half), BF),
            vmem((2, main, quarter), BF),
            vmem((2, slots, width), BF),
            vmem((2, 2, main, quarter), BF),
            vmem((width, hid), BF),
            vmem((width, hid), BF),
            vmem((hid, width), BF),
            vmem((slots, hid), F32),
            vmem((slots, hid), F32),
            vmem((slots, hid), BF),
            vmem((slots, hid), BF),
            vmem((slots, hid), BF),
            vmem((2, slots, half), BF),
            vmem((2, slots, half), BF),
            vmem((2, slots, half), BF),
            vmem((2, main, half), BF),
            vmem((2, main, quarter), BF),
            vmem((2, main, half), BF),
            vmem((2, main, quarter), BF),
            vmem((tok, main), BF),
            vmem((4, tok, main), BF),
            vmem((tok, 1), F32),
            vmem((2, tok // 2, half), BF),
            dma((2,)),
            dma((3,)),
            dma((2, experts, 2)),
            dma((2, experts, 2)),
            dma((2, experts, 2)),
            dma((2, experts, 2)),
            dma((2,)),
            dma((2,)),
            dma((2, experts, 2)),
            dma((2, experts, 2)),
            dma((2,)),
            dma((2,)),
        ],
        compiler_params=pltpu.CompilerParams(collective_id=0, has_side_effects=True, vmem_limit_bytes=60 << 20),
    )(
        expert_ids.reshape(1, tok),
        gate_weights.reshape(1, tok),
        layout_map.reshape(1, tok),
        tokens,
        grads_out,
        gate_w[0],
        up_w[0],
        down_w[0],
    )


def solution(mesh):
    in_specs = (
        P(("dp", "expert"), None),
        P(("dp", "expert"), None),
        P(("dp", "expert"), None),
        P(("dp", "expert"), None),
        P(("dp", "expert")),
        P("expert", None, "tensor"),
        P("expert", None, "tensor"),
        P("expert", "tensor", None),
    )
    out_specs = (P(("dp", "expert", "tensor"), None), P(("dp", "expert", "tensor"), None))
    return jax.shard_map(shards, mesh=mesh, in_specs=in_specs, out_specs=out_specs, check_vma=False)
```

```python
import functools

import jax
import jax.numpy as jnp
from jax import lax
from jax.experimental import pallas as pl
from jax.experimental.pallas import tpu as pltpu
from jax.sharding import PartitionSpec as P

MESH = pl.DeviceIdType.MESH
FAR_FIRST = (5, 3, 7, 4, 1, 2, 6)
BF, F32 = jnp.bfloat16, jnp.float32


def iota(shape, axis):
    return lax.broadcasted_iota(jnp.int32, shape, axis)


def dot(a, b):
    return jnp.dot(a, b, preferred_element_type=F32)


def dot_t(a, b):
    return lax.dot_general(a, b, (((1,), (1,)), ((), ())), preferred_element_type=F32)


def one_hot(mask):
    return jnp.where(mask, 1.0, 0.0).astype(BF)


def kernel(
    experts, cap,
    ids_hbm, gates_hbm, layout_hbm, tokens_ref, grads_ref, wg_hbm, wu_hbm, wd_hbm,
    out_ref, grad_ref,
    ids_ref, gates_ref, layout_ref, rows, send_main, send_left, x_all, left_all, wg, wu, wd,
    pre_gate, pre_up, hidden, grad_gate, grad_up, part_away, part_home, part_recv,
    back_main, back_left, home_main, home_left, pick_main, pick_left, gate_row, away_out,
    in_sem, w_sem, disp_s, disp_r, fwd_s, fwd_r, part_s, part_r, ret_s, ret_r, end_s, end_r,
):
    me, core = lax.axis_index("expert"), lax.axis_index("tensor")
    tok, width = tokens_ref.shape
    half = width // 2
    quarter = half // 4
    peers = experts - 1
    main = 16 * experts
    extra = cap - 16
    half_rows = tok // 2
    partner = {"tensor": 1 - core}
    mine = pl.multiple_of(core * half, 128)
    other = pl.multiple_of((1 - core) * half, 128)

    def peer(k):
        x, y = me // 2, me % 2
        return ((x + k // 2) % (experts // 2)) * 2 + (y + k) % 2

    def source(k):
        x, y = me // 2, me % 2
        return ((x + experts // 2 - k // 2) % (experts // 2)) * 2 + (y + k) % 2

    small = [
        pltpu.make_async_copy(ids_hbm, ids_ref, in_sem.at[2]),
        pltpu.make_async_copy(gates_hbm, gates_ref, in_sem.at[3]),
        pltpu.make_async_copy(layout_hbm, layout_ref, in_sem.at[4]),
    ]
    loads = [
        pltpu.make_async_copy(tokens_ref.at[:, pl.ds(mine, half)], rows.at[0], in_sem.at[0]),
        pltpu.make_async_copy(grads_ref.at[:, pl.ds(mine, half)], rows.at[1], in_sem.at[1]),
    ]
    weights = [
        pltpu.make_async_copy(wg_hbm, wg, w_sem.at[0]),
        pltpu.make_async_copy(wu_hbm, wu, w_sem.at[1]),
        pltpu.make_async_copy(wd_hbm, wd, w_sem.at[2]),
    ]
    for copy in [small[0], loads[0], *small[1:], loads[1]]:
        copy.start()
    barrier = pltpu.get_barrier_semaphore()
    for k in FAR_FIRST:
        pl.semaphore_signal(barrier, inc=1, device_id={"expert": peer(k)}, device_id_type=MESH)
    pl.semaphore_signal(barrier, inc=1, device_id=partner, device_id_type=MESH)
    for copy in small:
        copy.wait()

    ids = ids_ref[...]
    named = one_hot(iota((experts, tok), 0) == ids)
    earlier = one_hot(iota((tok, tok), 0) < iota((tok, tok), 1))
    rank = jnp.sum(dot(named, earlier) * named.astype(F32), axis=0, keepdims=True)
    base = ids.astype(F32) * 16.0
    row_id = iota((main, tok), 0).astype(F32)
    main_row = jnp.where(rank < 16.0, base + rank, -1.0)
    to_main = one_hot(row_id == main_row)
    to_left = []
    for q in range(4):
        left_row = jnp.where(rank < 16.0, -1.0, base + (rank - 16.0 + extra * q))
        to_left.append(one_hot(row_id == left_row))
    gates = gates_ref[...]
    same = iota((tok, tok), 0) == iota((tok, tok), 1)
    gate_col = jnp.sum(jnp.where(same, gates, 0.0), axis=1, keepdims=True)

    def dispatch(a, k):
        e = peer(k)
        here, there = pl.ds(pl.multiple_of(e * 16, 16), 16), pl.ds(pl.multiple_of(me * 16, 16), 16)
        return (
            pltpu.make_async_remote_copy(
                send_main.at[a, here], x_all.at[a, there, pl.ds(mine, half)],
                disp_s.at[a, k, 0], disp_r.at[a, k, 0], device_id={"expert": e}, device_id_type=MESH),
            pltpu.make_async_remote_copy(
                send_left.at[a, here], left_all.at[a, core, there],
                disp_s.at[a, k, 1], disp_r.at[a, k, 1], device_id={"expert": e}, device_id_type=MESH),
        )

    def forward(a, k):
        at = pl.ds(pl.multiple_of(source(k) * 16, 16), 16)
        return (
            pltpu.make_async_remote_copy(
                x_all.at[a, at, pl.ds(mine, half)], x_all.at[a, at, pl.ds(mine, half)],
                fwd_s.at[a, k, 0], fwd_r.at[a, k, 0], device_id=partner, device_id_type=MESH),
            pltpu.make_async_remote_copy(
                left_all.at[a, core, at], left_all.at[a, core, at],
                fwd_s.at[a, k, 1], fwd_r.at[a, k, 1], device_id=partner, device_id_type=MESH),
        )

    def arrange(a):
        left = jnp.zeros((main, quarter), F32)
        for q in range(4):
            cols = pl.ds(q * quarter, quarter)
            block = rows[a, :, cols]
            if a == 1:
                block = (block.astype(F32) * gate_col).astype(BF)
            send_main[a, :, cols] = dot(to_main, block).astype(BF)
            left = left + dot(to_left[q], block)
        send_left[a] = left.astype(BF)

    def send_all(a):
        for k in FAR_FIRST:
            for copy in dispatch(a, k):
                copy.start()
        own = pl.ds(pl.multiple_of(me * 16, 16), 16)
        x_all[a, own, pl.ds(mine, half)] = send_main[a, own]
        left_all[a, core, own] = send_left[a, own]

    def forward_all(a):
        for copy in forward(a, 0):
            copy.start()
        for k in reversed(FAR_FIRST):
            for copy in dispatch(a, k):
                copy.wait_recv()
            for copy in forward(a, k):
                copy.start()

    def forward_wait(a):
        for k in range(experts):
            for copy in forward(a, k):
                copy.wait_recv()

    def spread_left(a, h):
        r, c = iota((experts * extra, main), 0), iota((experts * extra, main), 1)
        for q in range(4):
            pick = one_hot(c == (r // extra) * 16 + q * extra + r % extra)
            at = pl.ds(pl.multiple_of(h * half + q * quarter, 128), quarter)
            x_all[a, main:, at] = dot(pick, left_all[a, h]).astype(BF)

    loads[0].wait()
    loads[1].wait()
    for copy in weights:
        copy.start()
    arrange(0)
    pl.semaphore_wait(barrier, peers + 1)
    send_all(0)
    arrange(1)

    place = one_hot(iota((tok, tok), 0) == layout_ref[...])
    pick_main[...] = dot_t(place, to_main).astype(BF)
    for q in range(4):
        pick_left[q] = dot_t(place, to_left[q]).astype(BF)
    gate_row[...] = jnp.sum(jnp.where(iota((tok, tok), 0) == layout_ref[...], gates, 0.0), axis=1, keepdims=True)

    for k in FAR_FIRST:
        for copy in dispatch(0, k):
            copy.wait_send()
    send_all(1)

    forward_all(0)
    for copy in weights:
        copy.wait()
    here, there = pl.ds(mine, half), pl.ds(other, half)
    spread_left(0, core)
    pre_gate[...] = dot(x_all[0, :, here], wg[here, :])
    pre_up[...] = dot(x_all[0, :, here], wu[here, :])
    forward_wait(0)
    spread_left(0, 1 - core)
    pre_gate[...] += dot(x_all[0, :, there], wg[there, :])
    pre_up[...] += dot(x_all[0, :, there], wu[there, :])
    hidden[...] = (pre_gate[...] * jax.nn.sigmoid(pre_gate[...]) * pre_up[...]).astype(BF)

    def exchange(a):
        return pltpu.make_async_remote_copy(
            part_away.at[a], part_recv.at[a], part_s.at[a], part_r.at[a], device_id=partner, device_id_type=MESH)

    def out_part(start, ref):
        for q in range(4):
            cols = pl.ds(q * quarter, quarter)
            ref[0, :, cols] = dot(hidden[...], wd[:, pl.ds(pl.multiple_of(start + q * quarter, 128), quarter)]).astype(BF)

    def grad_part(start, ref):
        for q in range(4):
            cols = pl.ds(q * quarter, quarter)
            at = pl.ds(pl.multiple_of(start + q * quarter, 128), quarter)
            ref[1, :, cols] = (dot_t(grad_gate[...], wg[at, :]) + dot_t(grad_up[...], wu[at, :])).astype(BF)

    def give_back(a, k):
        g = peer(k)
        here, there = pl.ds(pl.multiple_of(g * 16, 16), 16), pl.ds(pl.multiple_of(me * 16, 16), 16)
        return (
            pltpu.make_async_remote_copy(
                back_main.at[a, here], home_main.at[a, there],
                ret_s.at[a, k, 0], ret_r.at[a, k, 0], device_id={"expert": g}, device_id_type=MESH),
            pltpu.make_async_remote_copy(
                back_left.at[a, here], home_left.at[a, there],
                ret_s.at[a, k, 1], ret_r.at[a, k, 1], device_id={"expert": g}, device_id_type=MESH),
        )

    def return_all(a):
        exchange(a).wait_recv()
        r, c = iota((main, experts * extra), 0), iota((main, experts * extra), 1)
        packed = jnp.zeros((main, quarter), F32)
        for q in range(4):
            cols = pl.ds(q * quarter, quarter)
            total = (part_home[a, :, cols].astype(F32) + part_recv[a, :, cols].astype(F32)).astype(BF)
            back_main[a, :, cols] = total[:main]
            pick = one_hot(r == (c // extra) * 16 + q * extra + c % extra)
            packed = packed + dot(pick, total[main:])
        back_left[a] = packed.astype(BF)
        for k in FAR_FIRST:
            for copy in give_back(a, k):
                copy.start()
        own = pl.ds(pl.multiple_of(me * 16, 16), 16)
        home_main[a, own] = back_main[a, own]
        home_left[a, own] = back_left[a, own]

    out_part(other, part_away)
    exchange(0).start()
    out_part(mine, part_home)
    return_all(0)

    forward_all(1)
    spread_left(1, core)
    grad_hidden = dot_t(x_all[1, :, here], wd[:, here])
    forward_wait(1)
    spread_left(1, 1 - core)
    grad_hidden += dot_t(x_all[1, :, there], wd[:, there])
    gate_v, up_v = pre_gate[...], pre_up[...]
    sigma = jax.nn.sigmoid(gate_v)
    grad_gate[...] = (grad_hidden * up_v * sigma * (1.0 + gate_v * (1.0 - sigma))).astype(BF)
    grad_up[...] = (grad_hidden * gate_v * sigma).astype(BF)
    grad_part(other, part_away)
    exchange(1).start()
    grad_part(mine, part_home)
    return_all(1)

    def finish_copy(a, ref):
        return pltpu.make_async_remote_copy(
            away_out.at[a], ref.at[:, pl.ds(mine, half)], end_s.at[a], end_r.at[a],
            device_id=partner, device_id_type=MESH)

    keep = pl.ds(pl.multiple_of(core * half_rows, half_rows), half_rows)
    give = pl.ds(pl.multiple_of((1 - core) * half_rows, half_rows), half_rows)

    def finish(a, ref):
        for k in range(1, experts):
            for copy in give_back(a, k):
                copy.wait_recv()

        def placed(at, q):
            cols = pl.ds(q * quarter, quarter)
            value = dot(pick_main[at], home_main[a, :, cols]) + dot(pick_left[q, at], home_left[a])
            if a == 0:
                value = value * gate_row[at]
            return value.astype(BF)

        for q in range(4):
            away_out[a, :, pl.ds(q * quarter, quarter)] = placed(give, q)
        finish_copy(a, ref).start()
        for q in range(4):
            ref[:, pl.ds(pl.multiple_of(mine + q * quarter, 128), quarter)] = placed(keep, q)

    finish(0, out_ref)
    finish(1, grad_ref)

    for a, ref in ((0, out_ref), (1, grad_ref)):
        for k in range(1, experts):
            if a == 1:
                for copy in dispatch(a, k):
                    copy.wait_send()
            for copy in give_back(a, k):
                copy.wait_send()
        for k in range(experts):
            for copy in forward(a, k):
                copy.wait_send()
        exchange(a).wait_send()
        finish_copy(a, ref).wait()


def flush(a_ref, b_ref, a_hbm, b_hbm, sem):
    copies = [pltpu.make_async_copy(a_ref, a_hbm, sem.at[0]), pltpu.make_async_copy(b_ref, b_hbm, sem.at[1])]
    for copy in copies:
        copy.start()
    for copy in copies:
        copy.wait()


def shards(tokens, grads_out, expert_ids, gate_weights, layout_map, gate_w, up_w, down_w):
    tok, width = tokens.shape
    experts = lax.axis_size("expert")
    hid = gate_w.shape[2]
    cap = tok * 5 // (4 * experts)
    half = width // 2
    quarter = half // 4
    slots, main = experts * cap, experts * 16
    vmem, dma = pltpu.VMEM, pltpu.SemaphoreType.DMA
    in_vmem, anywhere = pl.BlockSpec(memory_space=pltpu.VMEM), pl.BlockSpec(memory_space=pl.ANY)
    out = jax.ShapeDtypeStruct((tok // 2, width), BF)
    placed = pl.pallas_call(
        functools.partial(kernel, experts, cap),
        out_shape=(vmem(out.shape, BF), vmem(out.shape, BF)),
        in_specs=[anywhere] * 8,
        out_specs=(in_vmem, in_vmem),
        scratch_shapes=[
            vmem((1, tok), jnp.int32),
            vmem((1, tok), F32),
            vmem((1, tok), jnp.int32),
            vmem((2, tok, half), BF),
            vmem((2, main, half), BF),
            vmem((2, main, quarter), BF),
            vmem((2, slots, width), BF),
            vmem((2, 2, main, quarter), BF),
            vmem((width, hid), BF),
            vmem((width, hid), BF),
            vmem((hid, width), BF),
            vmem((slots, hid), F32),
            vmem((slots, hid), F32),
            vmem((slots, hid), BF),
            vmem((slots, hid), BF),
            vmem((slots, hid), BF),
            vmem((2, slots, half), BF),
            vmem((2, slots, half), BF),
            vmem((2, slots, half), BF),
            vmem((2, main, half), BF),
            vmem((2, main, quarter), BF),
            vmem((2, main, half), BF),
            vmem((2, main, quarter), BF),
            vmem((tok, main), BF),
            vmem((4, tok, main), BF),
            vmem((tok, 1), F32),
            vmem((2, tok // 2, half), BF),
            dma((5,)),
            dma((3,)),
            dma((2, experts, 2)),
            dma((2, experts, 2)),
            dma((2, experts, 2)),
            dma((2, experts, 2)),
            dma((2,)),
            dma((2,)),
            dma((2, experts, 2)),
            dma((2, experts, 2)),
            dma((2,)),
            dma((2,)),
        ],
        compiler_params=pltpu.CompilerParams(collective_id=0, has_side_effects=True, vmem_limit_bytes=60 << 20),
    )(
        expert_ids.reshape(1, tok),
        gate_weights.reshape(1, tok),
        layout_map.reshape(1, tok),
        tokens,
        grads_out,
        gate_w[0],
        up_w[0],
        down_w[0],
    )
    return pl.pallas_call(
        flush,
        out_shape=(out, out),
        in_specs=[in_vmem, in_vmem],
        out_specs=(anywhere, anywhere),
        scratch_shapes=[dma((2,))],
    )(*(pltpu.with_memory_space_constraint(value, pltpu.VMEM) for value in placed))


def solution(mesh):
    in_specs = (
        P(("dp", "expert"), None),
        P(("dp", "expert"), None),
        P(("dp", "expert"), None),
        P(("dp", "expert"), None),
        P(("dp", "expert")),
        P("expert", None, "tensor"),
        P("expert", None, "tensor"),
        P("expert", "tensor", None),
    )
    out_specs = (P(("dp", "expert", "tensor"), None), P(("dp", "expert", "tensor"), None))
    return jax.shard_map(shards, mesh=mesh, in_specs=in_specs, out_specs=out_specs, check_vma=False)
```

```python
import functools

import jax
import jax.numpy as jnp
from jax import lax
from jax.experimental import pallas as pl
from jax.experimental.pallas import tpu as pltpu
from jax.sharding import PartitionSpec as P

MESH = pl.DeviceIdType.MESH
FAR_FIRST = (5, 3, 7, 4, 1, 2, 6)
BF, F32 = jnp.bfloat16, jnp.float32


def iota(shape, axis):
    return lax.broadcasted_iota(jnp.int32, shape, axis)


def dot(a, b):
    return jnp.dot(a, b, preferred_element_type=F32)


def dot_t(a, b):
    return lax.dot_general(a, b, (((1,), (1,)), ((), ())), preferred_element_type=F32)


def one_hot(mask):
    return jnp.where(mask, 1.0, 0.0).astype(BF)


def kernel(
    experts, cap,
    ids_hbm, gates_hbm, layout_hbm, tokens_ref, grads_ref, wg_hbm, wu_hbm, wd_hbm,
    out_ref, grad_ref,
    ids_ref, gates_ref, layout_ref, rows, send_main, send_left, x_all, left_all, wg, wu, wd,
    pre_gate, pre_up, hidden, grad_gate, grad_up, part_away, part_home, part_recv,
    back_main, back_left, home_main, home_left, pick_main, pick_left, gate_row, away_out, keep_out,
    in_sem, w_sem, disp_s, disp_r, fwd_s, fwd_r, part_s, part_r, ret_s, ret_r, end_s, end_r, end_l,
):
    me, core = lax.axis_index("expert"), lax.axis_index("tensor")
    tok, width = tokens_ref.shape
    half = width // 2
    quarter = half // 4
    peers = experts - 1
    main = 16 * experts
    extra = cap - 16
    half_rows = tok // 2
    partner = {"tensor": 1 - core}
    mine = pl.multiple_of(core * half, 128)
    other = pl.multiple_of((1 - core) * half, 128)

    def peer(k):
        x, y = me // 2, me % 2
        return ((x + k // 2) % (experts // 2)) * 2 + (y + k) % 2

    def source(k):
        x, y = me // 2, me % 2
        return ((x + experts // 2 - k // 2) % (experts // 2)) * 2 + (y + k) % 2

    small = [
        pltpu.make_async_copy(ids_hbm, ids_ref, in_sem.at[2]),
        pltpu.make_async_copy(gates_hbm, gates_ref, in_sem.at[3]),
        pltpu.make_async_copy(layout_hbm, layout_ref, in_sem.at[4]),
    ]
    loads = [
        pltpu.make_async_copy(tokens_ref.at[:, pl.ds(mine, half)], rows.at[0], in_sem.at[0]),
        pltpu.make_async_copy(grads_ref.at[:, pl.ds(mine, half)], rows.at[1], in_sem.at[1]),
    ]
    weights = [
        pltpu.make_async_copy(wg_hbm, wg, w_sem.at[0]),
        pltpu.make_async_copy(wu_hbm, wu, w_sem.at[1]),
        pltpu.make_async_copy(wd_hbm, wd, w_sem.at[2]),
    ]
    for copy in [small[0], loads[0], *small[1:], loads[1]]:
        copy.start()
    barrier = pltpu.get_barrier_semaphore()
    for k in FAR_FIRST:
        pl.semaphore_signal(barrier, inc=1, device_id={"expert": peer(k)}, device_id_type=MESH)
    pl.semaphore_signal(barrier, inc=1, device_id=partner, device_id_type=MESH)
    for copy in small:
        copy.wait()

    ids = ids_ref[...]
    named = one_hot(iota((experts, tok), 0) == ids)
    earlier = one_hot(iota((tok, tok), 0) < iota((tok, tok), 1))
    rank = jnp.sum(dot(named, earlier) * named.astype(F32), axis=0, keepdims=True)
    base = ids.astype(F32) * 16.0
    row_id = iota((main, tok), 0).astype(F32)
    main_row = jnp.where(rank < 16.0, base + rank, -1.0)
    to_main = one_hot(row_id == main_row)
    to_left = []
    for q in range(4):
        left_row = jnp.where(rank < 16.0, -1.0, base + (rank - 16.0 + extra * q))
        to_left.append(one_hot(row_id == left_row))
    gates = gates_ref[...]
    same = iota((tok, tok), 0) == iota((tok, tok), 1)
    gate_col = jnp.sum(jnp.where(same, gates, 0.0), axis=1, keepdims=True)

    def dispatch(a, k):
        e = peer(k)
        here, there = pl.ds(pl.multiple_of(e * 16, 16), 16), pl.ds(pl.multiple_of(me * 16, 16), 16)
        return (
            pltpu.make_async_remote_copy(
                send_main.at[a, here], x_all.at[a, there, pl.ds(mine, half)],
                disp_s.at[a, k, 0], disp_r.at[a, k, 0], device_id={"expert": e}, device_id_type=MESH),
            pltpu.make_async_remote_copy(
                send_left.at[a, here], left_all.at[a, core, there],
                disp_s.at[a, k, 1], disp_r.at[a, k, 1], device_id={"expert": e}, device_id_type=MESH),
        )

    def forward(a, k):
        at = pl.ds(pl.multiple_of(source(k) * 16, 16), 16)
        return (
            pltpu.make_async_remote_copy(
                x_all.at[a, at, pl.ds(mine, half)], x_all.at[a, at, pl.ds(mine, half)],
                fwd_s.at[a, k, 0], fwd_r.at[a, k, 0], device_id=partner, device_id_type=MESH),
            pltpu.make_async_remote_copy(
                left_all.at[a, core, at], left_all.at[a, core, at],
                fwd_s.at[a, k, 1], fwd_r.at[a, k, 1], device_id=partner, device_id_type=MESH),
        )

    def arrange(a):
        left = jnp.zeros((main, quarter), F32)
        for q in range(4):
            cols = pl.ds(q * quarter, quarter)
            block = rows[a, :, cols]
            if a == 1:
                block = (block.astype(F32) * gate_col).astype(BF)
            send_main[a, :, cols] = dot(to_main, block).astype(BF)
            left = left + dot(to_left[q], block)
        send_left[a] = left.astype(BF)

    def send_all(a):
        for k in FAR_FIRST:
            for copy in dispatch(a, k):
                copy.start()
        own = pl.ds(pl.multiple_of(me * 16, 16), 16)
        x_all[a, own, pl.ds(mine, half)] = send_main[a, own]
        left_all[a, core, own] = send_left[a, own]

    def forward_all(a):
        for copy in forward(a, 0):
            copy.start()
        for k in reversed(FAR_FIRST):
            for copy in dispatch(a, k):
                copy.wait_recv()
            for copy in forward(a, k):
                copy.start()

    def forward_wait(a):
        for k in range(experts):
            for copy in forward(a, k):
                copy.wait_recv()

    def spread_left(a, h):
        r, c = iota((experts * extra, main), 0), iota((experts * extra, main), 1)
        for q in range(4):
            pick = one_hot(c == (r // extra) * 16 + q * extra + r % extra)
            at = pl.ds(pl.multiple_of(h * half + q * quarter, 128), quarter)
            x_all[a, main:, at] = dot(pick, left_all[a, h]).astype(BF)

    loads[0].wait()
    loads[1].wait()
    for copy in weights:
        copy.start()
    arrange(0)
    pl.semaphore_wait(barrier, peers + 1)
    send_all(0)
    arrange(1)

    place = one_hot(iota((tok, tok), 0) == layout_ref[...])
    pick_main[...] = dot_t(place, to_main).astype(BF)
    for q in range(4):
        pick_left[q] = dot_t(place, to_left[q]).astype(BF)
    gate_row[...] = jnp.sum(jnp.where(iota((tok, tok), 0) == layout_ref[...], gates, 0.0), axis=1, keepdims=True)

    for copy in dispatch(0, FAR_FIRST[0]):
        copy.wait_send()
    send_all(1)

    forward_all(0)
    for copy in weights:
        copy.wait()
    here, there = pl.ds(mine, half), pl.ds(other, half)
    spread_left(0, core)
    pre_gate[...] = dot(x_all[0, :, here], wg[here, :])
    pre_up[...] = dot(x_all[0, :, here], wu[here, :])
    forward_wait(0)
    spread_left(0, 1 - core)
    pre_gate[...] += dot(x_all[0, :, there], wg[there, :])
    pre_up[...] += dot(x_all[0, :, there], wu[there, :])
    hidden[...] = (pre_gate[...] * jax.nn.sigmoid(pre_gate[...]) * pre_up[...]).astype(BF)

    def exchange(a, q):
        cols = pl.ds(q * quarter, quarter)
        return pltpu.make_async_remote_copy(
            part_away.at[a, :, cols], part_recv.at[a, :, cols], part_s.at[a, q], part_r.at[a, q],
            device_id=partner, device_id_type=MESH)

    def out_part(start, q):
        return dot(hidden[...], wd[:, pl.ds(pl.multiple_of(start + q * quarter, 128), quarter)]).astype(BF)

    def grad_part(start, q):
        at = pl.ds(pl.multiple_of(start + q * quarter, 128), quarter)
        return (dot_t(grad_gate[...], wg[at, :]) + dot_t(grad_up[...], wu[at, :])).astype(BF)

    def give_back(a, k):
        g = peer(k)
        here, there = pl.ds(pl.multiple_of(g * 16, 16), 16), pl.ds(pl.multiple_of(me * 16, 16), 16)
        return [
            pltpu.make_async_remote_copy(
                back_main.at[a, here, pl.ds(q * quarter, quarter)], home_main.at[a, there, pl.ds(q * quarter, quarter)],
                ret_s.at[a, k, q], ret_r.at[a, k, q], device_id={"expert": g}, device_id_type=MESH)
            for q in range(4)
        ] + [
            pltpu.make_async_remote_copy(
                back_left.at[a, here], home_left.at[a, there],
                ret_s.at[a, k, 4], ret_r.at[a, k, 4], device_id={"expert": g}, device_id_type=MESH)
        ]

    def return_all(a, part):
        r, c = iota((main, experts * extra), 0), iota((main, experts * extra), 1)
        packed = jnp.zeros((main, quarter), F32)
        for step in range(6):
            if step < 4:
                part_away[a, :, pl.ds(step * quarter, quarter)] = part(other, step)
                exchange(a, step).start()
            if 1 <= step < 5:
                part_home[a, :, pl.ds((step - 1) * quarter, quarter)] = part(mine, step - 1)
            if step >= 2:
                q = step - 2
                cols = pl.ds(q * quarter, quarter)
                exchange(a, q).wait_recv()
                total = (part_home[a, :, cols].astype(F32) + part_recv[a, :, cols].astype(F32)).astype(BF)
                back_main[a, :, cols] = total[:main]
                pick = one_hot(r == (c // extra) * 16 + q * extra + c % extra)
                packed = packed + dot(pick, total[main:])
                for k in FAR_FIRST:
                    give_back(a, k)[q].start()
        back_left[a] = packed.astype(BF)
        for k in FAR_FIRST:
            give_back(a, k)[4].start()
        own = pl.ds(pl.multiple_of(me * 16, 16), 16)
        home_main[a, own] = back_main[a, own]
        home_left[a, own] = back_left[a, own]

    return_all(0, out_part)

    forward_all(1)
    spread_left(1, core)
    grad_hidden = dot_t(x_all[1, :, here], wd[:, here])
    forward_wait(1)
    spread_left(1, 1 - core)
    grad_hidden += dot_t(x_all[1, :, there], wd[:, there])
    gate_v, up_v = pre_gate[...], pre_up[...]
    sigma = jax.nn.sigmoid(gate_v)
    grad_gate[...] = (grad_hidden * up_v * sigma * (1.0 + gate_v * (1.0 - sigma))).astype(BF)
    grad_up[...] = (grad_hidden * gate_v * sigma).astype(BF)
    return_all(1, grad_part)

    def finish_copy(a, ref):
        return pltpu.make_async_remote_copy(
            away_out.at[a], ref.at[:, pl.ds(mine, half)], end_s.at[a], end_r.at[a],
            device_id=partner, device_id_type=MESH)

    def keep_copy(a, ref):
        return pltpu.make_async_copy(keep_out.at[a], ref.at[:, pl.ds(mine, half)], end_l.at[a])

    keep = pl.ds(pl.multiple_of(core * half_rows, half_rows), half_rows)
    give = pl.ds(pl.multiple_of((1 - core) * half_rows, half_rows), half_rows)

    def finish(a, ref):
        for k in range(1, experts):
            for copy in give_back(a, k):
                copy.wait_recv()

        def placed(at, q):
            cols = pl.ds(q * quarter, quarter)
            value = dot(pick_main[at], home_main[a, :, cols]) + dot(pick_left[q, at], home_left[a])
            if a == 0:
                value = value * gate_row[at]
            return value.astype(BF)

        for q in range(4):
            away_out[a, :, pl.ds(q * quarter, quarter)] = placed(give, q)
        finish_copy(a, ref).start()
        for q in range(4):
            keep_out[a, :, pl.ds(q * quarter, quarter)] = placed(keep, q)
        keep_copy(a, ref).start()

    finish(0, out_ref)
    finish(1, grad_ref)

    for a, ref in ((0, out_ref), (1, grad_ref)):
        for k in range(1, experts):
            if a == 1 or k != FAR_FIRST[0]:
                for copy in dispatch(a, k):
                    copy.wait_send()
            for copy in give_back(a, k):
                copy.wait_send()
        for k in range(experts):
            for copy in forward(a, k):
                copy.wait_send()
        for q in range(4):
            exchange(a, q).wait_send()
        keep_copy(a, ref).wait()
        finish_copy(a, ref).wait()


def flush(a_ref, b_ref, a_hbm, b_hbm, sem):
    copies = [pltpu.make_async_copy(a_ref, a_hbm, sem.at[0]), pltpu.make_async_copy(b_ref, b_hbm, sem.at[1])]
    for copy in copies:
        copy.start()
    for copy in copies:
        copy.wait()


def shards(tokens, grads_out, expert_ids, gate_weights, layout_map, gate_w, up_w, down_w):
    tok, width = tokens.shape
    experts = lax.axis_size("expert")
    hid = gate_w.shape[2]
    cap = tok * 5 // (4 * experts)
    half = width // 2
    quarter = half // 4
    slots, main = experts * cap, experts * 16
    vmem, dma = pltpu.VMEM, pltpu.SemaphoreType.DMA
    anywhere = pl.BlockSpec(memory_space=pl.ANY)
    out = jax.ShapeDtypeStruct((tok // 2, width), BF)
    placed = pl.pallas_call(
        functools.partial(kernel, experts, cap),
        out_shape=(vmem(out.shape, BF), vmem(out.shape, BF)),
        in_specs=[anywhere] * 8,
        out_specs=(anywhere, anywhere),
        scratch_shapes=[
            vmem((1, tok), jnp.int32),
            vmem((1, tok), F32),
            vmem((1, tok), jnp.int32),
            vmem((2, tok, half), BF),
            vmem((2, main, half), BF),
            vmem((2, main, quarter), BF),
            vmem((2, slots, width), BF),
            vmem((2, 2, main, quarter), BF),
            vmem((width, hid), BF),
            vmem((width, hid), BF),
            vmem((hid, width), BF),
            vmem((slots, hid), F32),
            vmem((slots, hid), F32),
            vmem((slots, hid), BF),
            vmem((slots, hid), BF),
            vmem((slots, hid), BF),
            vmem((2, slots, half), BF),
            vmem((2, slots, half), BF),
            vmem((2, slots, half), BF),
            vmem((2, main, half), BF),
            vmem((2, main, quarter), BF),
            vmem((2, main, half), BF),
            vmem((2, main, quarter), BF),
            vmem((tok, main), BF),
            vmem((4, tok, main), BF),
            vmem((tok, 1), F32),
            vmem((2, tok // 2, half), BF),
            vmem((2, tok // 2, half), BF),
            dma((5,)),
            dma((3,)),
            dma((2, experts, 2)),
            dma((2, experts, 2)),
            dma((2, experts, 2)),
            dma((2, experts, 2)),
            dma((2, 4)),
            dma((2, 4)),
            dma((2, experts, 5)),
            dma((2, experts, 5)),
            dma((2,)),
            dma((2,)),
            dma((2,)),
        ],
        compiler_params=pltpu.CompilerParams(collective_id=0, has_side_effects=True, vmem_limit_bytes=60 << 20),
    )(
        expert_ids.reshape(1, tok),
        gate_weights.reshape(1, tok),
        layout_map.reshape(1, tok),
        tokens,
        grads_out,
        gate_w[0],
        up_w[0],
        down_w[0],
    )
    return pl.pallas_call(
        flush,
        out_shape=(out, out),
        in_specs=[anywhere, anywhere],
        out_specs=(anywhere, anywhere),
        scratch_shapes=[dma((2,))],
    )(*(pltpu.with_memory_space_constraint(value, pltpu.VMEM) for value in placed))


def solution(mesh):
    in_specs = (
        P(("dp", "expert"), None),
        P(("dp", "expert"), None),
        P(("dp", "expert"), None),
        P(("dp", "expert"), None),
        P(("dp", "expert")),
        P("expert", None, "tensor"),
        P("expert", None, "tensor"),
        P("expert", "tensor", None),
    )
    out_specs = (P(("dp", "expert", "tensor"), None), P(("dp", "expert", "tensor"), None))
    return jax.shard_map(shards, mesh=mesh, in_specs=in_specs, out_specs=out_specs, check_vma=False)
```
